32 devices in a mesh: dp: 8 (over z, y), tensor: 4 (over x, core).
Axes of the slice: x: 2, y: 2, z: 4, core: 2. Of those that a mesh axis runs over, the one named last changes fastest.
Arguments:
- train_weight: bfloat16 [1024, 8192], P('tensor'), may hold values from -0.0625 to 0.0625
- rollout_inputs: bfloat16 [4, 8, 8192], P(None, 'dp', 'tensor'), may hold values from -6 to 6
- positions: int32 [8], P('dp'), may hold values from 0 to 8191
- lengths: int32 [8], P('dp'), may hold values from 1 to 4096, as said below
- queries: bfloat16 [4, 32, 1024], P(None, ('dp', 'tensor')), may hold values from -6 to 6
- kv_cache: bfloat16 [32, 4096, 256], P(('dp', 'tensor')), may hold values from -200 to 200
- train_inputs: bfloat16 [8192, 8192], P('dp'), may hold values from -6 to 6
- advantages: float32 [8192], P('dp'), may hold values from -5 to 5
- key_grads: bfloat16 [1024, 8192], P('tensor', 'dp'), may hold values from -0.0625 to 0.0625
Outputs:
- new_kv: bfloat16 [4, 8, 1024], P(None, 'dp')
- attended: bfloat16 [4, 32, 1024], P(None, ('dp', 'tensor'))
- weight_grad: bfloat16 [1024, 8192], P('tensor')
The draws below stay inside these ranges and needn't reach their ends.
Inputs may be any that keep to these rules, and one draw needn't show every extreme that they name: `lengths`: row 0 holds 4096 valid positions and row 1 holds one.
All inputs are finite; a program needn't handle non-finite values.
Results may differ from the reference program's by a relative error of at most 0.0052.
Values may be sent and summed in bfloat16 or wider, within the bound.
No kernel may reach another device: no remote copies, remote signals or barrier semaphores. Data moves between devices by JAX's collectives and lax.ppermute only.
A program may use at most 64 MiB of HBM per device.

```python
import math
import jax
import jax.numpy as jnp
from jax import lax

D = 8192
HD = 128
KVH = 4
QPK = 8
STEPS = 4
L = 4096
ROW_DEV = 1
KVW = 1024
RG = 1
ROWS_REP = 1
RROWS = 8
CROWS = 32
TOKENS = 8192
N_DP = 8
N_TENSOR = 4


def shared_queries(key):
    values = jax.random.normal(jax.random.fold_in(key, 101), (STEPS, CROWS, QPK * HD), jnp.float32)
    return jnp.clip(values, -6.0, 6.0)


def draw_queries(key, part):
    return shared_queries(key).astype(jnp.bfloat16)


def draw_kv_cache(key, part):
    base = jax.random.normal(jax.random.fold_in(key, 202), (CROWS, L, 2 * HD), jnp.float32)
    base = jnp.clip(base, -6.0, 6.0)
    return base.astype(jnp.bfloat16)


def draw_lengths(key, part):
    values = jax.random.randint(jax.random.fold_in(key, 303), (RROWS,), 1, L + 1)
    values = values.at[0].set(L)
    values = values.at[1].set(1)
    return values.astype(jnp.int32)


def touch_ends(values, key, smallest, top_value):
    dims = values.shape
    index_at = [jax.random.randint(jax.random.fold_in(key, axis), (), 0, dims[axis]) for axis in range(len(dims))]
    values = values.at[tuple(index_at)].set(smallest)
    longest = dims.index(max(dims))
    index_at[longest] = (index_at[longest] + 1) % dims[longest]
    return values.at[tuple(index_at)].set(top_value)


def levels(stream_key, dims, shards, smallest, largest):
    def one(dim, parts):
        heights = jax.random.uniform(jax.random.fold_in(jax.random.fold_in(stream_key, 6), dim), (parts,), jnp.float32, smallest / len(shards), largest / len(shards))
        return jnp.repeat(jnp.exp(heights), dims[dim] // parts).reshape((-1,) + (1,) * (len(dims) - dim - 1))

    gain = one(*shards[0])
    for cut in shards[1:]:
        gain = gain * one(*cut)
    return gain


def gaussian(rng, shape, scale, reach, shards=(), held_as=jnp.bfloat16):
    result = scale * jax.random.normal(rng, shape, jnp.float32)
    if shards:
        result = result * levels(rng, shape, shards, -0.22, 0.18)
    return jnp.clip(result, -reach, reach).astype(held_as)


def setup_inputs(seed: int = 0) -> dict:
    seeds = jax.random.split(jax.random.key(seed), 10)
    train_weight = gaussian(seeds[0], (KVW, D), D ** -0.5, 0.0625, ((0, 4),))
    rollout_inputs = gaussian(seeds[1], (STEPS, RROWS, D), 1.0, 6.0, ((1, 8), (2, 4)))
    positions = touch_ends(jax.random.randint(seeds[2], (RROWS,), 0, 8192), jax.random.fold_in(seeds[2], 1), 0, 8191).astype(jnp.int32)
    lengths = draw_lengths(jax.random.fold_in(seeds[9], 71), 0)
    queries = draw_queries(jax.random.fold_in(seeds[9], 71), 0)
    kv_cache = draw_kv_cache(jax.random.fold_in(seeds[9], 71), 0)
    train_inputs = gaussian(seeds[6], (TOKENS, D), 1.0, 6.0, ((0, 8),))
    advantages = gaussian(seeds[7], (TOKENS,), 1.0, 5.0, ((0, 8),), jnp.float32)
    key_grads = gaussian(seeds[8], (KVW, TOKENS), TOKENS ** -0.5, 0.0625, ((0, 4), (1, 8)))
    return dict(train_weight=train_weight, rollout_inputs=rollout_inputs, positions=positions, lengths=lengths, queries=queries, kv_cache=kv_cache, train_inputs=train_inputs, advantages=advantages, key_grads=key_grads)


rope_base = 500000.0

def rotate_keys(kv_proj, positions):
    steps_count, row_count, _ = kv_proj.shape
    half_dim = HD // 2
    frequency = rope_base ** (-2.0 * jnp.arange(half_dim, dtype=jnp.float32) / HD)
    where_at = (positions[None, :] + jnp.arange(steps_count, dtype=jnp.int32)[:, None]).astype(jnp.float32)
    angles = where_at[:, :, None] * frequency[None, None, :]
    cosine = jnp.cos(angles)[:, :, None, :]
    sine_part = jnp.sin(angles)[:, :, None, :]
    key_part = kv_proj[:, :, :KVH * HD].reshape(steps_count, row_count, KVH, 2, half_dim)
    front_half = key_part[:, :, :, 0, :]
    back_half = key_part[:, :, :, 1, :]
    turned = jnp.stack([front_half * cosine - back_half * sine_part, back_half * cosine + front_half * sine_part], axis=3)
    return jnp.concatenate([turned.reshape(steps_count, row_count, KVH * HD), kv_proj[:, :, KVH * HD:]], axis=2)

def attend_block(query_block, cache_block, new_keys, new_values, live_length):
    steps_count, row_count, _ = query_block.shape
    heads_q = query_block.reshape(steps_count, row_count, QPK, HD).astype(jnp.float32)
    scale_by = 1.0 / math.sqrt(HD)
    cache_keys = cache_block[:, :, :HD].astype(jnp.float32)
    cache_values = cache_block[:, :, HD:].astype(jnp.float32)
    old_scores = jnp.einsum('srjd,rpd->srjp', heads_q, cache_keys) * scale_by
    fresh_scores = jnp.einsum('srjd,trd->srjt', heads_q, new_keys.astype(jnp.float32)) * scale_by
    cache_live = jnp.arange(cache_block.shape[1], dtype=jnp.int32)[None, :] < live_length[:, None]
    order = jnp.arange(steps_count, dtype=jnp.int32)
    fresh_live = order[None, :] <= order[:, None]
    old_masked = jnp.where(cache_live[None, :, None, :], old_scores, -jnp.inf)
    fresh_masked = jnp.where(fresh_live[:, None, None, :], fresh_scores, -jnp.inf)
    top = jnp.maximum(lax.optimization_barrier(jnp.max(old_masked, axis=3)), lax.optimization_barrier(jnp.max(fresh_masked, axis=3)))[..., None]
    old_weight = jnp.exp(old_masked - top)
    fresh_weight = jnp.exp(fresh_masked - top)
    total = lax.optimization_barrier(jnp.sum(old_weight, axis=3, keepdims=True)) + lax.optimization_barrier(jnp.sum(fresh_weight, axis=3, keepdims=True))
    old_share = (old_weight / total).astype(jnp.bfloat16).astype(jnp.float32)
    fresh_share = (fresh_weight / total).astype(jnp.bfloat16).astype(jnp.float32)
    mixed = jnp.einsum('srjp,rpd->srjd', old_share, cache_values)
    mixed = mixed + jnp.einsum('srjt,trd->srjd', fresh_share, new_values.astype(jnp.float32))
    return mixed.reshape(steps_count, row_count, QPK * HD).astype(jnp.bfloat16)

def reference(train_weight, rollout_inputs, positions, lengths, queries, kv_cache, train_inputs, advantages, key_grads):
    kv_proj = jnp.einsum('srd,kd->srk', rollout_inputs.astype(jnp.float32), train_weight.astype(jnp.float32))
    new_kv = rotate_keys(kv_proj, positions).astype(jnp.bfloat16)

    def one_device(device_rank):
        dp_rank = device_rank // N_TENSOR
        tensor_rank = device_rank % N_TENSOR
        head_index = tensor_rank // RG
        group_index = tensor_rank % RG
        cache_start = (device_rank * ROW_DEV).astype(jnp.int32)
        replica_start = (dp_rank * ROWS_REP + group_index * ROW_DEV).astype(jnp.int32)
        query_block = lax.dynamic_slice_in_dim(queries, cache_start, ROW_DEV, 1)
        cache_block = lax.dynamic_slice_in_dim(kv_cache, cache_start, ROW_DEV, 0)
        own_rows = lax.dynamic_slice_in_dim(new_kv, replica_start, ROW_DEV, 1)
        new_keys = lax.dynamic_slice_in_dim(own_rows, (head_index * HD).astype(jnp.int32), HD, 2)
        new_values = lax.dynamic_slice_in_dim(own_rows, (KVH * HD + head_index * HD).astype(jnp.int32), HD, 2)
        live_length = lax.dynamic_slice_in_dim(lengths, replica_start, ROW_DEV, 0)
        return attend_block(query_block, cache_block, new_keys, new_values, live_length)
    blocks = lax.map(one_device, jnp.arange(N_DP * N_TENSOR, dtype=jnp.int32))
    attended = jnp.transpose(blocks, (1, 0, 2, 3)).reshape(STEPS, CROWS, QPK * HD)
    scaled = (key_grads.astype(jnp.float32) * advantages[None, :]).astype(jnp.bfloat16)
    weight_grad = jnp.dot(scaled, train_inputs, preferred_element_type=jnp.float32).astype(jnp.bfloat16)
    return (new_kv, attended, weight_grad)
```

```python
import math

import jax
import jax.numpy as jnp
from jax import lax
from jax.sharding import PartitionSpec as P

HD = 128
KVH = 4
QPK = 8
LANES = 128


rope_base = 500000.0


def rotate_keys(kv_proj, positions):
    steps_count, row_count, _ = kv_proj.shape
    half_dim = HD // 2
    frequency = rope_base ** (-2.0 * jnp.arange(half_dim, dtype=jnp.float32) / HD)
    where_at = (positions[None, :] + jnp.arange(steps_count, dtype=jnp.int32)[:, None]).astype(
        jnp.float32
    )
    angles = where_at[:, :, None] * frequency[None, None, :]
    cosine = jnp.cos(angles)[:, :, None, :]
    sine_part = jnp.sin(angles)[:, :, None, :]
    key_part = kv_proj[:, :, : KVH * HD].reshape(steps_count, row_count, KVH, 2, half_dim)
    front_half = key_part[:, :, :, 0, :]
    back_half = key_part[:, :, :, 1, :]
    turned = jnp.stack(
        [front_half * cosine - back_half * sine_part, back_half * cosine + front_half * sine_part],
        axis=3,
    )
    return jnp.concatenate(
        [turned.reshape(steps_count, row_count, KVH * HD), kv_proj[:, :, KVH * HD :]], axis=2
    )


def attend_block(query_block, cache_block, new_keys, new_values, live_length):
    steps_count, row_count, _ = query_block.shape
    heads_q = query_block.reshape(steps_count, row_count, QPK, HD)
    scale_by = 1.0 / math.sqrt(HD)
    cache_keys = cache_block[:, :, :HD]
    cache_values = cache_block[:, :, HD:]
    old_scores = (
        jnp.einsum("srjd,rpd->srjp", heads_q, cache_keys, preferred_element_type=jnp.float32)
        * scale_by
    )
    fresh_scores = (
        jnp.einsum("srjd,trd->srjt", heads_q, new_keys, preferred_element_type=jnp.float32)
        * scale_by
    )
    cache_live = jnp.arange(cache_block.shape[1], dtype=jnp.int32)[None, :] < live_length[:, None]
    order = jnp.arange(steps_count, dtype=jnp.int32)
    fresh_live = order[None, :] <= order[:, None]
    old_masked = jnp.where(cache_live[None, :, None, :], old_scores, -jnp.inf)
    fresh_masked = jnp.where(fresh_live[:, None, None, :], fresh_scores, -jnp.inf)
    top = jnp.maximum(jnp.max(old_masked, axis=3), jnp.max(fresh_masked, axis=3))[..., None]
    old_weight = jnp.exp(old_masked - top)
    fresh_weight = jnp.exp(fresh_masked - top)
    total = jnp.sum(old_weight, axis=3, keepdims=True) + jnp.sum(
        fresh_weight, axis=3, keepdims=True
    )
    old_share = (old_weight / total).astype(jnp.bfloat16)
    fresh_share = (fresh_weight / total).astype(jnp.bfloat16)
    mixed = jnp.einsum(
        "srjp,rpd->srjd", old_share, cache_values, preferred_element_type=jnp.float32
    )
    mixed = mixed + jnp.einsum(
        "srjt,trd->srjd", fresh_share, new_values, preferred_element_type=jnp.float32
    )
    return mixed.reshape(steps_count, row_count, QPK * HD).astype(jnp.bfloat16)


def gather_small(value, axis_name, axis):
    count = lax.axis_size(axis_name)
    if count & (count - 1):
        return lax.all_gather(value, axis_name, axis=axis, tiled=True)
    rank = lax.axis_index(axis_name)
    bit = 1
    while bit < count:
        other = lax.ppermute(value, axis_name, [(i, i ^ bit) for i in range(count)])
        high = (rank // bit) % 2 == 1
        value = jnp.where(
            high,
            jnp.concatenate([other, value], axis=axis),
            jnp.concatenate([value, other], axis=axis),
        )
        bit *= 2
    return value


def ring_order(count):
    if count % 2:
        return list(range(count))
    return list(range(0, count, 2)) + list(range(count - 1, 0, -2))


def ring_rank(count):
    index = lax.axis_index("dp")
    if count % 2:
        return index
    return jnp.where(index % 2 == 0, index // 2, count - 1 - index // 2)


def ring_pairs(count, tensor_count, flip):
    order = ring_order(count)
    pairs = []
    for place in range(count):
        for member in range(tensor_count):
            step = 1 if (member + flip) % 2 == 0 else -1
            target = order[(place + step) % count]
            pairs.append((order[place] * tensor_count + member, target * tensor_count + member))
    return pairs


def summed_gradient(scaled, train_inputs):
    count = lax.axis_size("dp")
    tensor_count = lax.axis_size("tensor")
    column_count = train_inputs.shape[1]
    width = -(-column_count // (2 * count * LANES)) * LANES
    padded = 2 * count * width
    if padded != column_count:
        train_inputs = jnp.pad(train_inputs, ((0, 0), (0, padded - column_count)))
    place = ring_rank(count)
    parity = lax.axis_index("tensor") % 2
    streams = []
    for flip in range(2):
        forward = (parity + flip) % 2 == 0
        virtual = jnp.where(forward, place, (count - place) % count)
        streams.append((flip * count, virtual, ring_pairs(count, tensor_count, flip)))

    def chunk_of(stream, offset):
        first, virtual, _ = stream
        return (first + (virtual + offset + 2 * count) % count) * width

    def term_of(stream, offset, scaled):
        columns = lax.dynamic_slice_in_dim(train_inputs, chunk_of(stream, offset), width, 1)
        return jnp.dot(scaled, columns, preferred_element_type=jnp.float32)

    both = ("dp", "tensor")
    held = [term_of(stream, -1, scaled).astype(jnp.bfloat16) for stream in streams]
    for step in range(count - 1):
        for i, stream in enumerate(streams):
            sent, factor = lax.optimization_barrier((held[i], scaled))
            arrived = lax.ppermute(sent, both, stream[2])
            total = arrived.astype(jnp.float32) + term_of(stream, -2 - step, factor)
            held[i] = total.astype(jnp.bfloat16)
    result = jnp.zeros((scaled.shape[0], padded), jnp.bfloat16)
    for i, stream in enumerate(streams):
        result = lax.dynamic_update_slice_in_dim(result, held[i], chunk_of(stream, 0), 1)
    for step in range(count - 1):
        for i, stream in enumerate(streams):
            held[i] = lax.ppermute(held[i], both, stream[2])
            result = lax.dynamic_update_slice_in_dim(
                result, held[i], chunk_of(stream, -1 - step), 1
            )
    return result[:, :column_count]


def body(
    train_weight,
    rollout_inputs,
    positions,
    lengths,
    queries,
    kv_cache,
    train_inputs,
    advantages,
    key_grads,
):
    tensor_count = lax.axis_size("tensor")
    tensor_rank = lax.axis_index("tensor")
    group_count = tensor_count // KVH
    head_index = tensor_rank // group_count
    group_index = tensor_rank % group_count
    scaled = (key_grads.astype(jnp.float32) * advantages[None, :]).astype(jnp.bfloat16)
    weight_grad = summed_gradient(scaled, train_inputs)

    whole_inputs = gather_small(rollout_inputs, "tensor", 2)
    own_proj = jnp.einsum(
        "srd,kd->srk", whole_inputs, train_weight, preferred_element_type=jnp.float32
    )
    kv_proj = gather_small(own_proj, "tensor", 2)
    new_kv = rotate_keys(kv_proj, positions).astype(jnp.bfloat16)
    row_count = kv_cache.shape[0]
    row_start = group_index * row_count
    own_rows = lax.dynamic_slice_in_dim(new_kv, row_start, row_count, 1)
    new_keys = lax.dynamic_slice_in_dim(own_rows, head_index * HD, HD, 2)
    new_values = lax.dynamic_slice_in_dim(own_rows, KVH * HD + head_index * HD, HD, 2)
    live_length = lax.dynamic_slice_in_dim(lengths, row_start, row_count, 0)
    attended = attend_block(queries, kv_cache, new_keys, new_values, live_length)
    return (new_kv, attended, weight_grad)


def solution(mesh):
    return jax.shard_map(
        body,
        mesh=mesh,
        in_specs=(
            P("tensor", None),
            P(None, "dp", "tensor"),
            P("dp"),
            P("dp"),
            P(None, ("dp", "tensor"), None),
            P(("dp", "tensor"), None, None),
            P("dp", None),
            P("dp"),
            P("tensor", "dp"),
        ),
        out_specs=(P(None, "dp", None), P(None, ("dp", "tensor"), None), P("tensor", None)),
        check_vma=False,
    )
```

```python
import math

import jax
import jax.numpy as jnp
from jax import lax
from jax.sharding import PartitionSpec as P

HD = 128
KVH = 4
QPK = 8
LANES = 128


rope_base = 500000.0


def rotate_keys(kv_proj, positions):
    steps_count, row_count, _ = kv_proj.shape
    half_dim = HD // 2
    frequency = rope_base ** (-2.0 * jnp.arange(half_dim, dtype=jnp.float32) / HD)
    where_at = (positions[None, :] + jnp.arange(steps_count, dtype=jnp.int32)[:, None]).astype(
        jnp.float32
    )
    angles = where_at[:, :, None] * frequency[None, None, :]
    cosine = jnp.cos(angles)[:, :, None, :]
    sine_part = jnp.sin(angles)[:, :, None, :]
    key_part = kv_proj[:, :, : KVH * HD].reshape(steps_count, row_count, KVH, 2, half_dim)
    front_half = key_part[:, :, :, 0, :]
    back_half = key_part[:, :, :, 1, :]
    turned = jnp.stack(
        [front_half * cosine - back_half * sine_part, back_half * cosine + front_half * sine_part],
        axis=3,
    )
    return jnp.concatenate(
        [turned.reshape(steps_count, row_count, KVH * HD), kv_proj[:, :, KVH * HD :]], axis=2
    )


def attend_block(query_block, cache_block, new_keys, new_values, live_length):
    steps_count, row_count, _ = query_block.shape
    heads_q = query_block.reshape(steps_count, row_count, QPK, HD)
    scale_by = 1.0 / math.sqrt(HD)
    cache_keys = cache_block[:, :, :HD]
    cache_values = cache_block[:, :, HD:]
    old_scores = (
        jnp.einsum("srjd,rpd->srjp", heads_q, cache_keys, preferred_element_type=jnp.float32)
        * scale_by
    )
    fresh_scores = (
        jnp.einsum("srjd,trd->srjt", heads_q, new_keys, preferred_element_type=jnp.float32)
        * scale_by
    )
    cache_live = jnp.arange(cache_block.shape[1], dtype=jnp.int32)[None, :] < live_length[:, None]
    order = jnp.arange(steps_count, dtype=jnp.int32)
    fresh_live = order[None, :] <= order[:, None]
    old_masked = jnp.where(cache_live[None, :, None, :], old_scores, -jnp.inf)
    fresh_masked = jnp.where(fresh_live[:, None, None, :], fresh_scores, -jnp.inf)
    top = jnp.maximum(jnp.max(old_masked, axis=3), jnp.max(fresh_masked, axis=3))[..., None]
    old_weight = jnp.exp(old_masked - top)
    fresh_weight = jnp.exp(fresh_masked - top)
    total = jnp.sum(old_weight, axis=3, keepdims=True) + jnp.sum(
        fresh_weight, axis=3, keepdims=True
    )
    old_share = (old_weight / total).astype(jnp.bfloat16)
    fresh_share = (fresh_weight / total).astype(jnp.bfloat16)
    mixed = jnp.einsum(
        "srjp,rpd->srjd", old_share, cache_values, preferred_element_type=jnp.float32
    )
    mixed = mixed + jnp.einsum(
        "srjt,trd->srjd", fresh_share, new_values, preferred_element_type=jnp.float32
    )
    return mixed.reshape(steps_count, row_count, QPK * HD).astype(jnp.bfloat16)


def gather_small(value, axis_name, axis):
    count = lax.axis_size(axis_name)
    if count & (count - 1):
        return lax.all_gather(value, axis_name, axis=axis, tiled=True)
    rank = lax.axis_index(axis_name)
    bit = 1
    while bit < count:
        other = lax.ppermute(value, axis_name, [(i, i ^ bit) for i in range(count)])
        high = (rank // bit) % 2 == 1
        value = jnp.where(
            high,
            jnp.concatenate([other, value], axis=axis),
            jnp.concatenate([value, other], axis=axis),
        )
        bit *= 2
    return value


def ring_order(count):
    if count % 2:
        return list(range(count))
    return list(range(0, count, 2)) + list(range(count - 1, 0, -2))


def ring_rank(count):
    index = lax.axis_index("dp")
    if count % 2:
        return index
    return jnp.where(index % 2 == 0, index // 2, count - 1 - index // 2)


def ring_pairs(count, tensor_count, flip):
    order = ring_order(count)
    pairs = []
    for place in range(count):
        for member in range(tensor_count):
            step = 1 if (member + flip) % 2 == 0 else -1
            target = order[(place + step) % count]
            pairs.append((order[place] * tensor_count + member, target * tensor_count + member))
    return pairs


def body(
    train_weight,
    rollout_inputs,
    positions,
    lengths,
    queries,
    kv_cache,
    train_inputs,
    advantages,
    key_grads,
):
    tensor_count = lax.axis_size("tensor")
    tensor_rank = lax.axis_index("tensor")
    count = lax.axis_size("dp")
    scaled = (key_grads.astype(jnp.float32) * advantages[None, :]).astype(jnp.bfloat16)

    column_count = train_inputs.shape[1]
    half = -(-column_count // (2 * count * LANES)) * LANES
    width = 2 * half
    padded = count * width
    if padded != column_count:
        train_inputs = jnp.pad(train_inputs, ((0, 0), (0, padded - column_count)))
    row_total = scaled.shape[0]
    place = ring_rank(count)
    both = ("dp", "tensor")
    pairs = [ring_pairs(count, tensor_count, flip) for flip in range(2)]
    sign = jnp.where(tensor_rank % 2 == 0, 1, -1)
    signs = [sign, -sign]
    hops = count // 2
    split = count % 2 == 0

    def chunk_at(stream, offset):
        return lax.rem(place + signs[stream] * offset + 2 * count, count)

    def term_of(factor, start, size):
        columns = lax.dynamic_slice_in_dim(train_inputs, start, size, 1)
        return jnp.dot(factor, columns, preferred_element_type=jnp.float32)

    rollout = {"inputs": rollout_inputs}

    def stage(number):
        if number == 0:
            rollout["inputs"] = gather_small(rollout["inputs"], "tensor", 2)
        elif number == 1:
            rollout["proj"] = jnp.einsum(
                "srd,kd->srk", rollout["inputs"], train_weight, preferred_element_type=jnp.float32
            )
        elif number == 2:
            rollout["proj"] = gather_small(rollout["proj"], "tensor", 2)
        else:
            rollout["out"] = finish_rollout(
                rollout["proj"], positions, lengths, queries, kv_cache, tensor_rank, tensor_count
            )

    def tied(sent, stage_number=None, factor=None):
        key = "inputs" if stage_number in (0, 1) else "proj"
        values = [sent]
        if factor is not None:
            values.append(factor)
        if stage_number is not None:
            values.append(rollout[key])
        values = list(lax.optimization_barrier(tuple(values)))
        if stage_number is not None:
            rollout[key] = values.pop()
            stage(stage_number)
        return values

    own_start = place * width
    far_start = [chunk_at(stream, hops) * width for stream in range(2)]
    held = []
    for stream in range(2):
        if split:
            first = jnp.where(signs[stream] > 0, 0, half)
            term = term_of(scaled, far_start[stream] + first, half)
        else:
            term = term_of(scaled, far_start[stream], width)
        held.append(term.astype(jnp.bfloat16))
    stages = {(1, 0): 0, (2, 0): 1}
    for hop in range(hops):
        left = hops - 1 - hop
        for stream in range(2):
            sent, factor = tied(held[stream], stages.get((hop, stream)), scaled)
            arrived = lax.ppermute(sent, both, pairs[stream]).astype(jnp.float32)
            if left == 0:
                held[stream] = arrived
                continue
            term = term_of(factor, chunk_at(stream, left) * width, width)
            if hop == 0 and split:
                first = signs[stream] > 0
                low = term[:, :half] + jnp.where(first, arrived, 0.0)
                high = term[:, half:] + jnp.where(first, 0.0, arrived)
                total = jnp.concatenate([low, high], axis=1)
            else:
                total = term + arrived
            held[stream] = total.astype(jnp.bfloat16)
    if hops == 0:
        own = term_of(scaled, own_start, width)
    else:
        own = term_of(factor, own_start, width)
        if hops == 1 and split:
            first = signs[0] > 0
            low = jnp.where(first, held[0], held[1])
            high = jnp.where(first, held[1], held[0])
            own = own + jnp.concatenate([low, high], axis=1)
        else:
            own = own + held[0] + held[1]
    own = own.astype(jnp.bfloat16)
    result = jnp.zeros((row_total, padded), jnp.bfloat16)
    result = lax.dynamic_update_slice_in_dim(result, own, own_start, 1)
    held = [own, own]
    stages = {(1, 0): 2, (2, 0): 3}
    for hop in range(hops):
        for stream in range(2):
            start = chunk_at(stream, -1 - hop) * width
            last = hop == hops - 1 and split
            sent = held[stream]
            if last:
                first = signs[stream] > 0
                sent = jnp.where(first, sent[:, :half], sent[:, half:])
                start = start + jnp.where(first, 0, half)
            (sent,) = tied(sent, stages.get((hop, stream)))
            held[stream] = lax.ppermute(sent, both, pairs[stream])
            result = lax.dynamic_update_slice_in_dim(result, held[stream], start, 1)
    new_kv, attended = rollout["out"]
    return (new_kv, attended, result[:, :column_count])


def finish_rollout(kv_proj, positions, lengths, queries, kv_cache, tensor_rank, tensor_count):
    group_count = tensor_count // KVH
    head_index = tensor_rank // group_count
    group_index = tensor_rank % group_count
    new_kv = rotate_keys(kv_proj, positions).astype(jnp.bfloat16)
    row_count = kv_cache.shape[0]
    row_start = group_index * row_count
    own_rows = lax.dynamic_slice_in_dim(new_kv, row_start, row_count, 1)
    new_keys = lax.dynamic_slice_in_dim(own_rows, head_index * HD, HD, 2)
    new_values = lax.dynamic_slice_in_dim(own_rows, KVH * HD + head_index * HD, HD, 2)
    live_length = lax.dynamic_slice_in_dim(lengths, row_start, row_count, 0)
    return new_kv, attend_block(queries, kv_cache, new_keys, new_values, live_length)


def solution(mesh):
    return jax.shard_map(
        body,
        mesh=mesh,
        in_specs=(
            P("tensor", None),
            P(None, "dp", "tensor"),
            P("dp"),
            P("dp"),
            P(None, ("dp", "tensor"), None),
            P(("dp", "tensor"), None, None),
            P("dp", None),
            P("dp"),
            P("tensor", "dp"),
        ),
        out_specs=(P(None, "dp", None), P(None, ("dp", "tensor"), None), P("tensor", None)),
        check_vma=False,
    )
```

```python
import math

import jax
import jax.numpy as jnp
from jax import lax
from jax.experimental import pallas as pl
from jax.experimental.pallas import tpu as pltpu
from jax.sharding import PartitionSpec as P


HD = 128
KVH = 4
QPK = 8
LANES = 128


rope_base = 500000.0


def rotate_keys(kv_proj, positions):
    steps_count, row_count, _ = kv_proj.shape
    half_dim = HD // 2
    frequency = rope_base ** (-2.0 * jnp.arange(half_dim, dtype=jnp.float32) / HD)
    where_at = (positions[None, :] + jnp.arange(steps_count, dtype=jnp.int32)[:, None]).astype(
        jnp.float32
    )
    angles = where_at[:, :, None] * frequency[None, None, :]
    cosine = jnp.cos(angles)[:, :, None, :]
    sine_part = jnp.sin(angles)[:, :, None, :]
    key_part = kv_proj[:, :, : KVH * HD].reshape(steps_count, row_count, KVH, 2, half_dim)
    front_half = key_part[:, :, :, 0, :]
    back_half = key_part[:, :, :, 1, :]
    turned = jnp.stack(
        [front_half * cosine - back_half * sine_part, back_half * cosine + front_half * sine_part],
        axis=3,
    )
    return jnp.concatenate(
        [turned.reshape(steps_count, row_count, KVH * HD), kv_proj[:, :, KVH * HD :]], axis=2
    )


def attend_block(query_block, cache_block, new_keys, new_values, live_length):
    steps_count, row_count, _ = query_block.shape
    heads_q = query_block.reshape(steps_count, row_count, QPK, HD)
    scale_by = 1.0 / math.sqrt(HD)
    cache_keys = cache_block[:, :, :HD]
    cache_values = cache_block[:, :, HD:]
    old_scores = (
        jnp.einsum("srjd,rpd->srjp", heads_q, cache_keys, preferred_element_type=jnp.float32)
        * scale_by
    )
    fresh_scores = (
        jnp.einsum("srjd,trd->srjt", heads_q, new_keys, preferred_element_type=jnp.float32)
        * scale_by
    )
    cache_live = jnp.arange(cache_block.shape[1], dtype=jnp.int32)[None, :] < live_length[:, None]
    order = jnp.arange(steps_count, dtype=jnp.int32)
    fresh_live = order[None, :] <= order[:, None]
    old_masked = jnp.where(cache_live[None, :, None, :], old_scores, -jnp.inf)
    fresh_masked = jnp.where(fresh_live[:, None, None, :], fresh_scores, -jnp.inf)
    top = jnp.maximum(jnp.max(old_masked, axis=3), jnp.max(fresh_masked, axis=3))[..., None]
    old_weight = jnp.exp(old_masked - top)
    fresh_weight = jnp.exp(fresh_masked - top)
    total = jnp.sum(old_weight, axis=3, keepdims=True) + jnp.sum(
        fresh_weight, axis=3, keepdims=True
    )
    old_share = (old_weight / total).astype(jnp.bfloat16)
    fresh_share = (fresh_weight / total).astype(jnp.bfloat16)
    mixed = jnp.einsum(
        "srjp,rpd->srjd", old_share, cache_values, preferred_element_type=jnp.float32
    )
    mixed = mixed + jnp.einsum(
        "srjt,trd->srjd", fresh_share, new_values, preferred_element_type=jnp.float32
    )
    return mixed.reshape(steps_count, row_count, QPK * HD).astype(jnp.bfloat16)


def gather_small(value, axis_name, axis):
    count = lax.axis_size(axis_name)
    if count & (count - 1):
        return lax.all_gather(value, axis_name, axis=axis, tiled=True)
    rank = lax.axis_index(axis_name)
    bit = 1
    while bit < count:
        other = lax.ppermute(value, axis_name, [(i, i ^ bit) for i in range(count)])
        high = (rank // bit) % 2 == 1
        value = jnp.where(
            high,
            jnp.concatenate([other, value], axis=axis),
            jnp.concatenate([value, other], axis=axis),
        )
        bit *= 2
    return value


def ring_order(count):
    if count % 2:
        return list(range(count))
    return list(range(0, count, 2)) + list(range(count - 1, 0, -2))


def ring_rank(count):
    index = lax.axis_index("dp")
    if count % 2:
        return index
    return jnp.where(index % 2 == 0, index // 2, count - 1 - index // 2)


def ring_pairs(count, step):
    order = ring_order(count)
    return [(order[i], order[(i + step) % count]) for i in range(count)]


def spread_order(hop, hops, split):
    if hop == hops - 1 and split:
        return [(0, 0), (1, 1)]
    return [(0, 0), (1, 1), (0, 1), (1, 0)]


def place_chunks(parts, index, column_count):
    row_count, part = parts[0].shape
    width = part * len(parts)

    def kernel(index_ref, *refs):
        *part_refs, result_ref, done = refs
        copies = []
        for i, part_ref in enumerate(part_refs):
            columns = pl.ds(pl.multiple_of(index_ref[0] * width + i * part, part), part)
            copies.append(pltpu.make_async_copy(part_ref, result_ref.at[:, columns], done.at[i]))
        for copy in copies:
            copy.start()
        for copy in copies:
            copy.wait()

    return pl.pallas_call(
        kernel,
        out_shape=jax.ShapeDtypeStruct((row_count, column_count), parts[0].dtype),
        in_specs=[pl.BlockSpec(memory_space=pltpu.SMEM)]
        + [pl.BlockSpec(memory_space=pltpu.VMEM)] * len(parts),
        out_specs=pl.BlockSpec(memory_space=pl.ANY),
        scratch_shapes=[pltpu.SemaphoreType.DMA((len(parts),))],
        cost_estimate=pl.CostEstimate(
            flops=0, bytes_accessed=4 * row_count * width, transcendentals=0
        ),
        name="place_chunks",
    )(index.reshape(1).astype(jnp.int32), *parts)


def body(
    train_weight,
    rollout_inputs,
    positions,
    lengths,
    queries,
    kv_cache,
    train_inputs,
    advantages,
    key_grads,
):
    tensor_count = lax.axis_size("tensor")
    tensor_rank = lax.axis_index("tensor")
    count = lax.axis_size("dp")
    scaled = (key_grads.astype(jnp.float32) * advantages[None, :]).astype(jnp.bfloat16)

    column_count = train_inputs.shape[1]
    half = -(-column_count // (2 * count * LANES)) * LANES
    width = 2 * half
    padded = count * width
    if padded != column_count:
        train_inputs = jnp.pad(train_inputs, ((0, 0), (0, padded - column_count)))
    place = ring_rank(count)
    steps = (1, -1)
    pairs = [ring_pairs(count, step) for step in steps]
    hops = count // 2
    split = count % 2 == 0

    def chunk_at(stream, offset):
        return lax.rem(place + steps[stream] * offset + count, count) * width

    def term_of(start, size):
        columns = lax.dynamic_slice_in_dim(train_inputs, start, size, 1)
        return jnp.dot(scaled, columns, preferred_element_type=jnp.float32)

    rollout = {"inputs": rollout_inputs}

    def stage(number):
        if number == 0:
            rollout["inputs"] = gather_small(rollout["inputs"], "tensor", 2)
        elif number == 1:
            rollout["proj"] = jnp.einsum(
                "srd,kd->srk", rollout["inputs"], train_weight, preferred_element_type=jnp.float32
            )
        elif number == 2:
            rollout["proj"] = gather_small(rollout["proj"], "tensor", 2)
        else:
            rollout["out"] = finish_rollout(
                rollout["proj"], positions, lengths, queries, kv_cache, tensor_rank, tensor_count
            )

    def tied(sent, number):
        if number is None:
            return sent
        key = "inputs" if number in (0, 1) else "proj"
        sent, rollout[key] = lax.optimization_barrier((sent, rollout[key]))
        stage(number)
        return sent

    def widened(stream, part):
        zero = jnp.zeros((part.shape[0], width - part.shape[1]), part.dtype)
        return jnp.concatenate([part, zero] if stream == 0 else [zero, part], axis=1)

    held = []
    for stream in range(2):
        start = chunk_at(stream, hops)
        term = term_of(start + stream * half, half) if split else term_of(start, width)
        held.append(term.astype(jnp.bfloat16))
    stages = {(1, 0): 0, (2, 0): 1, (3, 0): 2}
    for hop in range(hops):
        left = hops - 1 - hop
        arrived = []
        for stream in range(2):
            sent = tied(held[stream], stages.pop((hop, stream), None))
            arrived.append(lax.ppermute(sent, "dp", pairs[stream]).astype(jnp.float32))
        if hop == 0 and split:
            arrived = [widened(stream, arrived[stream]) for stream in range(2)]
        terms = []
        for stream in range(2 if left > 0 else 1):
            term = term_of(chunk_at(stream, left), width)
            terms.append(lax.optimization_barrier(term))
        if left > 0:
            held = [(terms[i] + arrived[i]).astype(jnp.bfloat16) for i in range(2)]
        else:
            own = (terms[0] + arrived[0] + arrived[1]).astype(jnp.bfloat16)
    if hops == 0:
        own = term_of(place * width, width).astype(jnp.bfloat16)
    for number in stages.values():
        stage(number)
    own = lax.optimization_barrier((own[:, :half], own[:, half:]))
    result = place_chunks(own, place, padded)
    held = {(stream, group): own[group] for stream in range(2) for group in range(2)}
    finish = (1, 0, 1)
    for hop in range(hops):
        moves = spread_order(hop, hops, split)
        for stream, group in moves:
            sent = held[stream, group]
            if (hop, stream, group) == finish:
                sent = tied(sent, 3)
            held[stream, group] = lax.ppermute(sent, "dp", pairs[stream])
        for stream in range(2):
            groups = sorted(group for other, group in moves if other == stream)
            start = chunk_at(stream, -1 - hop) + groups[0] * half
            parts = [held[stream, group] for group in groups]
            part = jnp.concatenate(parts, axis=1) if len(parts) > 1 else parts[0]
            result = lax.dynamic_update_slice_in_dim(result, part, start, 1)
    if "out" not in rollout:
        stage(3)
    new_kv, attended = rollout["out"]
    return (new_kv, attended, result[:, :column_count])


def finish_rollout(kv_proj, positions, lengths, queries, kv_cache, tensor_rank, tensor_count):
    group_count = tensor_count // KVH
    head_index = tensor_rank // group_count
    group_index = tensor_rank % group_count
    new_kv = rotate_keys(kv_proj, positions).astype(jnp.bfloat16)
    row_count = kv_cache.shape[0]
    row_start = group_index * row_count
    own_rows = lax.dynamic_slice_in_dim(new_kv, row_start, row_count, 1)
    new_keys = lax.dynamic_slice_in_dim(own_rows, head_index * HD, HD, 2)
    new_values = lax.dynamic_slice_in_dim(own_rows, KVH * HD + head_index * HD, HD, 2)
    live_length = lax.dynamic_slice_in_dim(lengths, row_start, row_count, 0)
    return new_kv, attend_block(queries, kv_cache, new_keys, new_values, live_length)


def solution(mesh):
    return jax.shard_map(
        body,
        mesh=mesh,
        in_specs=(
            P("tensor", None),
            P(None, "dp", "tensor"),
            P("dp"),
            P("dp"),
            P(None, ("dp", "tensor"), None),
            P(("dp", "tensor"), None, None),
            P("dp", None),
            P("dp"),
            P("tensor", "dp"),
        ),
        out_specs=(P(None, "dp", None), P(None, ("dp", "tensor"), None), P("tensor", None)),
        check_vma=False,
    )
```
